256 devices in a mesh: rep: 32 (over z, y), tp: 8 (over x, core).
Axes of the slice: x: 4, y: 4, z: 8, core: 2. Of those that a mesh axis runs over, the one named last changes fastest.
Arguments:
- image_grads: bfloat16 [512, 48, 1280], P('rep', 'tp'), may hold values from -6 to 6
- dest_rank: int32 [512], P('rep'), may hold values from 0 to 31, as said below
- dest_slot: int32 [512], P('rep'), may hold values from 0 to 31, as said below
- saved_inputs: bfloat16 [1024, 48, 1280], P('rep'), may hold values from -6 to 6
- up_weight: bfloat16 [1280, 5120], P(None, 'tp'), may hold values from -0.15625 to 0.15625
- down_weight: bfloat16 [5120, 1280], P('tp'), may hold values from -0.078125 to 0.078125
- norm_gain: float32 [1280], replicated, may hold values from 0.25 to 1.75
Outputs:
- input_grads: bfloat16 [1024, 48, 1280], P('rep', 'tp')
- up_grads: float32 [1280, 5120], P('rep', 'tp')
- down_grads: float32 [5120, 1280], P('tp', 'rep')
- gain_grads: float32 [1280], replicated
The draws below stay inside these ranges and needn't reach their ends.
Inputs may be any that keep to these rules, and one draw needn't show every extreme that they name: `dest_rank`: the images of one index of rep go to different owners; each owner receives at most 32 images, and some owner receives exactly 32 in every draw. `dest_slot`: the images that one owner receives have distinct slots 0, 1, ... up to their count less one; other slots hold no image.
All inputs are finite; a program needn't handle non-finite values.
Results may differ from the reference program's by a relative error of at most 0.015.
Values may be sent and summed in bfloat16 or wider, within the bound.
A program may use at most 128 MiB of HBM per device.

```python
import jax
import jax.numpy as jnp
from jax import lax

D = 1280
FF = 5120
PATCH = 48
IMG_DEV = 16
ENC_CAP = 32
IMAGES = 512
ENC_SLOTS = 1024
N_REP = 32


def assignment(key):
    base = jax.random.fold_in(key, 4242)
    key_order, key_moves, key_source = jax.random.split(base, 3)
    half = N_REP // 2
    order = jax.random.permutation(key_order, N_REP)
    moves = jax.random.randint(key_moves, (half,), 0, IMG_DEV + 1)
    moves = moves.at[0].set(IMG_DEV)
    counts = jnp.zeros((N_REP,), jnp.int32)
    counts = counts.at[order[0::2]].add(IMG_DEV + moves)
    counts = counts.at[order[1::2]].add(IMG_DEV - moves)
    ends = jnp.cumsum(counts)
    starts = ends - counts
    entries = jnp.arange(IMG_DEV * N_REP, dtype=jnp.int32)
    owner = jnp.sum((entries[:, None] >= ends[None, :]).astype(jnp.int32), axis=1)
    position = entries - starts[owner]
    sources = jax.random.permutation(key_source, N_REP)
    source = sources[entries % N_REP]
    within = entries // N_REP
    index = source * IMG_DEV + within
    rank_out = jnp.zeros((IMG_DEV * N_REP,), jnp.int32).at[index].set(owner)
    slot_out = jnp.zeros((IMG_DEV * N_REP,), jnp.int32).at[index].set(position)
    return (rank_out, slot_out)


def draw_dest_rank(key, part):
    return assignment(key)[0]


def draw_dest_slot(key, part):
    return assignment(key)[1]


def shard_levels(own_key, dims, cuts, least, largest):
    loudness = 1.0
    for dim, shards_of in cuts:
        steps = jax.random.uniform(jax.random.fold_in(jax.random.fold_in(own_key, 6), dim), (shards_of,), jnp.float32, least / len(cuts), largest / len(cuts))
        loudness = loudness * jnp.repeat(jnp.exp(steps), dims[dim] // shards_of).reshape((-1,) + (1,) * (len(dims) - 1 - dim))
    return loudness


def gaussian(rng, dims, deviation, bound, cuts=(), held_as=jnp.bfloat16):
    loudness = shard_levels(rng, dims, cuts, -0.22, 0.18) if cuts else 1.0
    array = jax.random.normal(rng, dims, jnp.float32) * deviation * loudness
    return jnp.minimum(jnp.maximum(array, -bound), bound).astype(held_as)


def setup_inputs(seed: int = 0) -> dict:
    arg_keys = jax.random.split(jax.random.key(seed), 8)
    return {
        "image_grads": gaussian(arg_keys[0], (IMAGES, PATCH, D), 1.0, 6.0, ((0, 32), (1, 8))),
        "dest_rank": draw_dest_rank(jax.random.fold_in(arg_keys[7], 71), 0),
        "dest_slot": draw_dest_slot(jax.random.fold_in(arg_keys[7], 71), 0),
        "saved_inputs": gaussian(arg_keys[3], (ENC_SLOTS, PATCH, D), 1.0, 6.0, ((0, 32),)),
        "up_weight": gaussian(arg_keys[4], (D, FF), D ** -0.5, 0.15625, ((1, 8),)),
        "down_weight": gaussian(arg_keys[5], (FF, D), FF ** -0.5, 0.078125, ((0, 8),)),
        "norm_gain": jnp.clip(1.0 + 0.15 * jax.random.normal(arg_keys[6], (D,), jnp.float32), 0.25, 1.75),
    }


epsilon = 1e-05
gelu_c = 0.7978845608028654
gelu_a = 0.044715

def gelu_value(preact):
    inner = jnp.tanh(gelu_c * (preact + gelu_a * preact ** 3))
    return 0.5 * preact * (1.0 + inner)

def gelu_slope(preact):
    inner = jnp.tanh(gelu_c * (preact + gelu_a * preact ** 3))
    return 0.5 * (1.0 + inner) + 0.5 * preact * (1.0 - inner * inner) * gelu_c * (1.0 + 3.0 * gelu_a * preact * preact)

def reference(image_grads, dest_rank, dest_slot, saved_inputs, up_weight, down_weight, norm_gain):
    target = (dest_rank * ENC_CAP + dest_slot).astype(jnp.int32)
    routed = jnp.zeros((ENC_SLOTS, PATCH, D), jnp.bfloat16).at[target].set(image_grads)
    rows = ENC_CAP * PATCH
    saved_blocks = saved_inputs.reshape(N_REP, rows, D)
    routed_blocks = routed.reshape(N_REP, rows, D)

    def one_block(carry, pieces):
        up_acc, down_acc, gain_acc = carry
        inputs, grads = pieces
        values = inputs.astype(jnp.float32)
        mean_v = lax.optimization_barrier(jnp.mean(values, axis=1, keepdims=True))
        var_v = lax.optimization_barrier(jnp.mean((values - mean_v) ** 2, axis=1, keepdims=True))
        inv_std = 1.0 / jnp.sqrt(var_v + epsilon)
        centred = (values - mean_v) * inv_std
        normed = (centred * norm_gain[None, :]).astype(jnp.bfloat16)
        preact = jnp.dot(normed, up_weight, preferred_element_type=jnp.float32)
        hidden = gelu_value(preact).astype(jnp.bfloat16)
        grad_hidden = jnp.dot(grads, down_weight.T, preferred_element_type=jnp.float32)
        grad_pre = (grad_hidden * gelu_slope(preact)).astype(jnp.bfloat16)
        down_acc = down_acc + jnp.dot(hidden.T, grads, preferred_element_type=jnp.float32)
        up_acc = up_acc + jnp.dot(normed.T, grad_pre, preferred_element_type=jnp.float32)
        grad_normed = jnp.dot(grad_pre, up_weight.T, preferred_element_type=jnp.float32)
        gain_acc = gain_acc + lax.optimization_barrier(jnp.sum(grad_normed * centred, axis=0))
        scaled = grad_normed * norm_gain[None, :]
        first = lax.optimization_barrier(jnp.mean(scaled, axis=1, keepdims=True))
        second = lax.optimization_barrier(jnp.mean(scaled * centred, axis=1, keepdims=True))
        result = grads.astype(jnp.float32) + inv_std * (scaled - first - centred * second)
        return ((up_acc, down_acc, gain_acc), result.astype(jnp.bfloat16))
    start = (jnp.zeros((D, FF), jnp.float32), jnp.zeros((FF, D), jnp.float32), jnp.zeros((D,), jnp.float32))
    (up_grads, down_grads, gain_grads), outs = lax.scan(one_block, start, (saved_blocks, routed_blocks))
    input_grads = outs.reshape(ENC_SLOTS, PATCH, D)
    return (input_grads, up_grads, down_grads, gain_grads)
```

```python
import functools

import jax
import jax.numpy as jnp
from jax import lax
from jax.experimental import pallas as pl
from jax.experimental.pallas import tpu as pltpu
from jax.sharding import PartitionSpec as P

MESH = pl.DeviceIdType.MESH
bf16, f32 = jnp.bfloat16, jnp.float32

epsilon = 1e-05
gelu_c = 0.7978845608028654
gelu_a = 0.044715

N_REP, N_TP = 32, 8
NX, NY, NZ = 4, 4, 8
IMG, CAP, SLAB, D, FFL = 16, 32, 6, 1280, 640
SROWS = SLAB * CAP
HALF = SROWS // 2
ROWS = SROWS * N_TP
MSG = 1024
TAIL = D - MSG
VMEM_BYTES = 62 * 1024 * 1024


def wrap(value, n):
    return lax.rem(value + n, n)


def place():
    rep, tp = lax.axis_index("rep"), lax.axis_index("tp")
    z, y = rep // NY, lax.rem(rep, NY)
    x, core = tp // 2, lax.rem(tp, 2)
    return rep, tp, z, y, x, core


def greet(peers):
    barrier = pltpu.get_barrier_semaphore()
    for peer in peers:
        pl.semaphore_signal(barrier, inc=1, device_id=peer, device_id_type=MESH)
    return lambda: pl.semaphore_wait(barrier, len(peers))


def remote(src, dst, sems, index, device):
    return pltpu.make_async_remote_copy(
        src_ref=src,
        dst_ref=dst,
        send_sem=sems[0].at[index],
        recv_sem=sems[1].at[index],
        device_id=device,
        device_id_type=MESH,
    )


def iota(shape, dim):
    return lax.broadcasted_iota(jnp.int32, shape, dim)


def pick(mask):
    return jnp.where(mask, 1.0, 0.0).astype(bf16)


def dot(a, b):
    return jnp.dot(a, b, preferred_element_type=f32)


def pack(img_ref, rank_ref, slot_ref, packed):
    rows, cols = N_REP * 8, SLAB * IMG
    row, col = iota((rows, cols), 0), iota((rows, cols), 1)
    owner = (row // 8) == rank_ref[...]
    part, patch = lax.rem(row, 8), col // IMG
    main = pick(owner & (part == patch))
    tail = img_ref[:, MSG:]
    for j in range(3):
        q = pick(owner & (part >= SLAB) & (patch == 3 * (part - SLAB) + j))
        block = dot(main, img_ref[:, j * TAIL : (j + 1) * TAIL]) + dot(q, tail)
        packed[:, j * TAIL : (j + 1) * TAIL] = block.astype(bf16)
    mark = jnp.where(owner & (part == SLAB) & (patch == 0), slot_ref[...] + 1, 0)
    mark = jnp.sum(mark.astype(f32), axis=1, keepdims=True)
    block = dot(main, img_ref[:, 3 * TAIL : MSG]) + mark
    packed[:, 3 * TAIL :] = block.astype(bf16)


def unpack(inbound, store):
    rows = N_REP * 8
    row, col = iota((rows, rows), 0), iota((rows, rows), 1)
    marks = jnp.where(
        (lax.rem(row, 8) == SLAB) & (row // 8 == col // 8), inbound[:, 3 * TAIL :], 0.0
    ).astype(bf16)
    ones = jnp.ones((SROWS, rows), bf16)
    slots = dot(ones, marks)
    row, col = iota((SROWS, rows), 0), iota((SROWS, rows), 1)
    here = slots == (lax.rem(row, CAP) + 1).astype(f32)
    part, patch = lax.rem(col, 8), row // CAP
    main = pick(here & (part == patch))
    tail = jnp.zeros((SROWS, TAIL), f32)
    for j in range(3):
        q = pick(here & (part >= SLAB) & (patch == 3 * (part - SLAB) + j))
        tail = tail + dot(q, inbound[:, j * TAIL : (j + 1) * TAIL])
    store(dot(main, inbound[...]).astype(bf16), tail.astype(bf16))


def dispatch_kernel(img_ref, rank_ref, slot_ref, out, packed, inbound, ds, dr, xs, xr, cs, cr, ls):
    rep, tp, z, y, x, core = place()
    right = (rep, wrap(x + 1, NX) * 2 + core)
    left = (rep, wrap(x - 1, NX) * 2 + core)
    partner = (rep, x * 2 + 1 - core)
    others = [(wrap(rep + i, N_REP), tp) for i in range(1, N_REP)]
    entered = greet(others + [right, left, partner])
    pack(img_ref, rank_ref, slot_ref, packed)
    entered()

    def message(i, peer):
        return remote(
            packed.at[pl.ds(peer * 8, 8)], inbound.at[pl.ds(rep * 8, 8)], (ds, dr), i, (peer, tp)
        )

    def send(i, _):
        message(i, wrap(rep + i, N_REP)).start()
        return 0

    lax.fori_loop(1, N_REP, send, 0)
    own = pltpu.make_async_copy(packed.at[pl.ds(rep * 8, 8)], inbound.at[pl.ds(rep * 8, 8)], ls)
    own.start()
    own.wait()

    def finish(i, _):
        message(i, wrap(rep + i, N_REP)).wait()
        return 0

    lax.fori_loop(1, N_REP, finish, 0)

    def rows(slab, half):
        return out.at[pl.ds(pl.multiple_of(slab * SROWS + half * HALF, HALF), HALF)]

    def keep(main, tail):
        at = pl.ds(pl.multiple_of(tp * SROWS, SROWS), SROWS)
        out[at, :MSG] = main
        out[at, MSG:] = tail

    unpack(inbound, keep)

    def across(i, slab, half, peer):
        return remote(rows(slab, half), rows(slab, half), (xs, xr), i, peer)

    def beside(i, slab, half):
        return remote(rows(slab, half), rows(slab, half), (cs, cr), i, partner)

    lslab, rslab = wrap(x - 1, NX) * 2 + core, wrap(x + 1, NX) * 2 + core
    oslab = wrap(x + 2, NX) * 2 + core
    sent = []

    def go(copy):
        copy.start()
        sent.append(copy)

    go(across(0, tp, 0, right))
    go(across(1, tp, 1, left))
    go(across(2, tp, 1, right))
    go(across(3, tp, 0, left))
    go(beside(0, tp, 0))
    go(beside(1, tp, 1))
    across(0, lslab, 0, right).wait_recv()
    go(across(4, lslab, 0, right))
    go(beside(2, lslab, 0))
    across(1, rslab, 1, left).wait_recv()
    go(across(5, rslab, 1, left))
    go(beside(3, rslab, 1))
    across(2, lslab, 1, right).wait_recv()
    go(beside(4, lslab, 1))
    across(3, rslab, 0, left).wait_recv()
    go(beside(5, rslab, 0))
    across(4, oslab, 0, right).wait_recv()
    go(beside(6, oslab, 0))
    across(5, oslab, 1, left).wait_recv()
    go(beside(7, oslab, 1))
    flip = 1 - 2 * core
    for i, (slab, half) in enumerate(
        [(tp, 0), (tp, 1), (lslab, 0), (rslab, 1), (lslab, 1), (rslab, 0), (oslab, 0), (oslab, 1)]
    ):
        beside(i, slab + flip, half).wait_recv()
    for copy in sent:
        copy.wait_send()


def dispatch(images, dest_rank, dest_slot):
    flat = images.transpose(1, 0, 2).reshape(SLAB * IMG, D)
    rank = jnp.tile(dest_rank, SLAB)[None, :]
    slot = jnp.tile(dest_slot, SLAB)[None, :]
    dma = pltpu.SemaphoreType.DMA
    return pl.pallas_call(
        dispatch_kernel,
        out_shape=jax.ShapeDtypeStruct((ROWS, D), bf16),
        in_specs=[pl.BlockSpec(memory_space=pltpu.VMEM)] * 3,
        out_specs=pl.BlockSpec(memory_space=pltpu.VMEM),
        scratch_shapes=[
            pltpu.VMEM((N_REP * 8, MSG), bf16),
            pltpu.VMEM((N_REP * 8, MSG), bf16),
            dma((N_REP,)),
            dma((N_REP,)),
            dma((6,)),
            dma((6,)),
            dma((8,)),
            dma((8,)),
            dma,
        ],
        compiler_params=pltpu.CompilerParams(
            collective_id=0, has_side_effects=True, vmem_limit_bytes=VMEM_BYTES
        ),
        name="dispatch",
    )(flat, rank, slot)


def add(*terms):
    total = terms[0].astype(f32)
    for term in terms[1:]:
        total = total + term.astype(f32)
    return total


def reduce_kernel(
    part, up, down, gain, gn_out, up_out, down_out, gain_out,
    pr, q, tfar, tnear,
    ua, uacc, uin, ufar, uw, uzi, uzs,
    dzi, dzs, dw, dfar, dacc, din,
    gbuf, ss, rs,
):
    rep, tp, z, y, x, core = place()
    me = (rep, tp)
    partner = (rep, x * 2 + 1 - core)
    xr, xl = (rep, wrap(x + 1, NX) * 2 + core), (rep, wrap(x - 1, NX) * 2 + core)

    def at_y(k):
        return (z * NY + wrap(y + k, NY), tp)

    def at_z(k):
        return (wrap(z + k, NZ) * NY + y, tp)

    tps = [(rep, wrap(tp + i, N_TP)) for i in range(1, N_TP)]
    ys = [at_y(i) for i in range(1, NY)]
    zs = [at_z(i) for i in range(1, NZ)]
    entered = greet(tps + ys + zs)
    sent = []
    waits = {}
    count = [0]

    def go(key, src, dst, device):
        copy = remote(src, dst, (ss, rs), count[0], device)
        count[0] += 1
        copy.start()
        sent.append(copy)
        waits[key] = copy

    def got(key):
        waits[key].wait_recv()

    A, B = pl.ds(0, HALF), pl.ds(HALF, HALF)
    entered()

    def slab(k, half):
        start = pl.multiple_of(k * SROWS + half * HALF, HALF)
        return pl.ds(start, HALF)

    order = [wrap(x + 2, NX), wrap(x + 1, NX), wrap(x - 1, NX), x]
    for i, to in enumerate(order):
        for h in range(2):
            go(("pair", i, h), part.at[slab(to * 2 + 1 - core, h)], pr.at[i, h], partner)
    ylo, yhi = pl.ds(0, NZ // 2), pl.ds(NZ // 2, NZ // 2)
    yfar, yright, yleft = wrap(y + 2, NY), wrap(y + 1, NY), wrap(y - 1, NY)
    go("u0r", up.at[ylo, yfar], ufar.at[0], at_y(1))
    go("u0l", up.at[yhi, yfar], ufar.at[1], at_y(-1))
    go("u1r", up.at[yhi, yright], uin.at[0, yhi], at_y(1))
    go("u1l", up.at[ylo, yleft], uin.at[1, ylo], at_y(-1))
    dfirst = wrap(z + 4, NZ)
    go("d0r", down.at[dfirst, pl.ds(0, 2)], dzi.at[0, 0, pl.ds(0, 2)], at_z(1))
    go("d0l", down.at[dfirst, pl.ds(2, 2)], dzi.at[1, 0, pl.ds(2, 2)], at_z(-1))
    gbuf[0, 0] = gain[...]
    for i in range(1, N_TP):
        go(("g0", i), gbuf.at[0, 0], gbuf.at[0, i], tps[i - 1])

    def pair_sum(i, to):
        for h in range(2):
            got(("pair", i, h))
            q[i, h] = add(part[slab(to * 2 + core, h), :], pr[i, h]).astype(bf16)

    pair_sum(0, order[0])
    go("t0r", q.at[0, 0], tfar.at[0], xr)
    go("t0l", q.at[0, 1], tfar.at[1], xl)
    pair_sum(1, order[1])
    go("t1r", q.at[1, 1], tnear.at[0, 1], xr)
    pair_sum(2, order[2])
    go("t1l", q.at[2, 0], tnear.at[1, 0], xl)

    def down_step(k):
        for side, sign in ((0, 1), (1, -1)):
            name = "rl"[side]
            got(f"d{k - 1}{name}")
            to = wrap(z + sign * (4 - k), NZ)
            if k == 1:
                near, other = (pl.ds(0, 2), pl.ds(2, 2)) if side == 0 else (pl.ds(2, 2), pl.ds(0, 2))
                dzs[side, 0, near] = add(down[to, near], dzi[side, 0, near]).astype(bf16)
                dzs[side, 0, other] = down[to, other]
            else:
                dzs[side, k - 1] = add(down[to], dzi[side, k - 1]).astype(bf16)
            go(f"d{k}{name}", dzs.at[side, k - 1], dzi.at[side, k], at_z(sign))

    down_step(1)
    got("u0r")
    uacc[0] = add(up[ylo, yright], ufar[0]).astype(bf16)
    go("u2r", uacc.at[0], uin.at[0, ylo], at_y(1))
    got("u0l")
    uacc[1] = add(up[yhi, yleft], ufar[1]).astype(bf16)
    go("u2l", uacc.at[1], uin.at[1, yhi], at_y(-1))
    got("t0r")
    q[1, 0] = add(q[1, 0], tfar[0]).astype(bf16)
    go("t2r", q.at[1, 0], tnear.at[0, 0], xr)
    got("t0l")
    q[2, 1] = add(q[2, 1], tfar[1]).astype(bf16)
    go("t2l", q.at[2, 1], tnear.at[1, 1], xl)
    for i in range(1, N_TP):
        got(("g0", i))
    gbuf[1, 0] = jnp.sum(gbuf[0], axis=0)
    for i in range(1, NY):
        go(("g1", i), gbuf.at[1, 0], gbuf.at[1, i], ys[i - 1])
    down_step(2)
    for key in ("u1r", "u1l", "u2r", "u2l"):
        got(key)
    uw[...] = add(up[:, y], uin[0], uin[1]).astype(bf16)
    lo, hi = pl.ds(0, 24), pl.ds(24, 16)
    ufirst = wrap(z + 4, NZ)
    go("z0r", uw.at[ufirst, lo], uzi.at[0, 0, lo], at_z(1))
    go("z0l", uw.at[ufirst, hi], uzi.at[1, 0, hi], at_z(-1))
    down_step(3)

    def up_step(k):
        for side, sign in ((0, 1), (1, -1)):
            name = "rl"[side]
            got(f"z{k - 1}{name}")
            to = wrap(z + sign * (4 - k), NZ)
            if k == 1:
                near, other = (lo, hi) if side == 0 else (hi, lo)
                uzs[side, 0, near] = add(uw[to, near], uzi[side, 0, near]).astype(bf16)
                uzs[side, 0, other] = uw[to, other]
            else:
                uzs[side, k - 1] = add(uw[to], uzi[side, k - 1]).astype(bf16)
            go(f"z{k}{name}", uzs.at[side, k - 1], uzi.at[side, k], at_z(sign))

    up_step(1)
    for i in range(1, NY):
        got(("g1", i))
    gbuf[2, 0] = gbuf[1, 0] + gbuf[1, 1] + gbuf[1, 2] + gbuf[1, 3]
    for i in range(1, NZ):
        go(("g2", i), gbuf.at[2, 0], gbuf.at[2, i], zs[i - 1])
    up_step(2)
    got("d3r")
    got("d3l")
    dw[...] = add(down[z], dzi[0, 3], dzi[1, 3]).astype(bf16)
    go("e0r", dw.at[yfar, lo], dfar.at[0, lo], at_y(1))
    go("e0l", dw.at[yfar, hi], dfar.at[1, hi], at_y(-1))
    go("e1r", dw.at[yright, hi], din.at[0, hi], at_y(1))
    go("e1l", dw.at[yleft, lo], din.at[1, lo], at_y(-1))
    up_step(3)
    pair_sum(3, order[3])
    for key in ("t1r", "t1l", "t2r", "t2l"):
        got(key)
    for h in range(2):
        gn_out[pl.ds(h * HALF, HALF), :] = add(q[3, h], tnear[0, h], tnear[1, h])
    got("e0r")
    dacc[lo] = add(dw[yright, lo], dfar[0, lo]).astype(bf16)
    go("e2r", dacc.at[lo], din.at[0, lo], at_y(1))
    got("e0l")
    dacc[hi] = add(dw[yleft, hi], dfar[1, hi]).astype(bf16)
    go("e2l", dacc.at[hi], din.at[1, hi], at_y(-1))
    got("z3r")
    got("z3l")
    up_out[...] = add(uw[z], uzi[0, 3], uzi[1, 3])
    for key in ("e1r", "e1l", "e2r", "e2l"):
        got(key)
    down_out[...] = add(dw[y], din[0], din[1])
    for i in range(1, NZ):
        got(("g2", i))
    gain_out[...] = jnp.sum(gbuf[2], axis=0)
    for copy in sent:
        copy.wait_send()


N_COPIES = 8 + 4 + 2 + 7 + 2 + 2 + 2 + 2 + 2 + 3 + 2 + 2 + 2 + 2 + 7 + 2 + 4 + 2 + 2 + 8


def reduce_all(part, up, down, gain):
    dma = pltpu.SemaphoreType.DMA
    shape = jax.ShapeDtypeStruct
    vm = pltpu.VMEM
    return pl.pallas_call(
        reduce_kernel,
        out_shape=[shape((SROWS, D), f32), shape((40, FFL), f32), shape((40, FFL), f32), shape((1, D), f32)],
        in_specs=[pl.BlockSpec(memory_space=pltpu.VMEM)] * 4,
        out_specs=[pl.BlockSpec(memory_space=pltpu.VMEM)] * 4,
        scratch_shapes=[
            vm((4, 2, HALF, D), bf16), vm((4, 2, HALF, D), bf16), vm((2, HALF, D), bf16), vm((2, 2, HALF, D), bf16),
            vm((8, 128), f32), vm((2, 4, 40, FFL), bf16), vm((2, NZ, 40, FFL), bf16), vm((2, 4, 40, FFL), bf16),
            vm((NZ, 40, FFL), bf16), vm((2, 4, 40, FFL), bf16), vm((2, 3, 40, FFL), bf16),
            vm((2, 4, NY, 40, FFL), bf16), vm((2, 3, NY, 40, FFL), bf16), vm((NY, 40, FFL), bf16),
            vm((2, 40, FFL), bf16), vm((40, FFL), bf16), vm((2, 40, FFL), bf16),
            vm((3, 8, 1, D), f32),
            dma((N_COPIES,)), dma((N_COPIES,)),
        ],
        compiler_params=pltpu.CompilerParams(
            collective_id=1, has_side_effects=True, vmem_limit_bytes=VMEM_BYTES
        ),
        name="reduce_all",
    )(part, up.reshape(NZ, NY, 40, FFL), down.reshape(NZ, NY, 40, FFL), gain)


def gelu_parts(preact):
    inner = jnp.tanh(gelu_c * (preact + gelu_a * preact**3))
    value = 0.5 * preact * (1.0 + inner)
    slope = 0.5 * (1.0 + inner) + 0.5 * preact * (1.0 - inner * inner) * gelu_c * (
        1.0 + 3.0 * gelu_a * preact * preact
    )
    return value, slope


def normalise(values):
    values = values.astype(f32)
    mean_v = jnp.mean(values, axis=1, keepdims=True)
    var_v = jnp.mean((values - mean_v) ** 2, axis=1, keepdims=True)
    inv_std = 1.0 / jnp.sqrt(var_v + epsilon)
    return (values - mean_v) * inv_std, inv_std


def local(image_grads, dest_rank, dest_slot, saved_inputs, up_weight, down_weight, norm_gain):
    grads = dispatch(image_grads, dest_rank, dest_slot)
    values = saved_inputs.transpose(1, 0, 2).reshape(ROWS, D)
    centred, _ = normalise(values)
    normed = (centred * norm_gain[None, :]).astype(bf16)
    preact = dot(normed, up_weight)
    value, slope = gelu_parts(preact)
    hidden = value.astype(bf16)
    grad_hidden = dot(grads, down_weight.T)
    grad_pre = (grad_hidden * slope).astype(bf16)
    down_local = dot(grads.T, hidden)
    up_local = dot(normed.T, grad_pre)
    partial_normed = dot(grad_pre, up_weight.T).astype(bf16)
    gain_local = jnp.sum(up_local * up_weight.astype(f32), axis=1) / norm_gain
    slab_normed, up_grads, down_grads, gain_grads = reduce_all(
        partial_normed, up_local.astype(bf16), down_local.astype(bf16), gain_local[None, :]
    )
    start = lax.axis_index("tp") * SROWS
    own = lax.dynamic_slice_in_dim(grads, start, SROWS, 0).astype(f32)
    start = lax.axis_index("tp") * SLAB
    own_x = lax.dynamic_slice_in_dim(saved_inputs, start, SLAB, 1)
    centred, inv_std = normalise(own_x.transpose(1, 0, 2).reshape(SROWS, D))
    scaled = slab_normed * norm_gain[None, :]
    first = jnp.mean(scaled, axis=1, keepdims=True)
    second = jnp.mean(scaled * centred, axis=1, keepdims=True)
    result = (own + inv_std * (scaled - first - centred * second)).astype(bf16)
    input_grads = result.reshape(SLAB, CAP, D).transpose(1, 0, 2)
    return (input_grads, up_grads, down_grads.T, gain_grads[0])


def solution(mesh):
    return jax.shard_map(
        local,
        mesh=mesh,
        in_specs=(
            P("rep", "tp", None),
            P("rep"),
            P("rep"),
            P("rep", None, None),
            P(None, "tp"),
            P("tp", None),
            P(),
        ),
        out_specs=(P("rep", "tp", None), P("rep", "tp"), P("tp", "rep"), P()),
        check_vma=False,
    )
```
